32 devices in a mesh: group: 1, chan: 32 (over z, y, x, core).
Axes of the slice: x: 2, y: 2, z: 4, core: 2. Of those that a mesh axis runs over, the one named last changes fastest.
Arguments:
- records: bfloat16 [8, 128, 16384], P('group', None, 'chan'), may hold values from -6 to 6
- valid_flags: int32 [8, 128], P('group', 'chan'), may hold values 0 or 1
- source_ids: int32 [64], P('group'), may hold values from 0 to 127, as said below
Outputs:
- correlations: float32 [64, 128, 1001], P('group', 'chan')
The draws below stay inside these ranges and needn't reach their ends.
Inputs may be any that keep to these rules, and one draw needn't show every extreme that they name: `source_ids`: 64 distinct channel indices.
All inputs are finite; a program needn't handle non-finite values. No bound on the sum of `valid_flags` on one device may be relied on, other than what follows from the above.
Results may differ from the reference program's by a relative error of at most 0.00035.
The reference program's roundings to bfloat16 on the way count: a program that leaves them out, or rounds other values in their place, can miss the bound.
Values may be sent and summed in bfloat16 or wider, within the bound.
A program may use at most 64 MiB of HBM per device.

```python
import math
import jax
import jax.numpy as jnp
from jax import lax

SEGS = 8
WINDOW_TICKS = 16384
BAND = 600
SOURCES = 64
HALF_LAG = 500
CHANNELS = 128


noise_scale = 0.3


envelope_scale = 1.4


def draw_source_ids(key, part):
    inner = jax.random.permutation(key, CHANNELS - 2)[:SOURCES - 2].astype(jnp.int32) + 1
    ends = jnp.array([0, CHANNELS - 1], dtype=jnp.int32)
    joined = jnp.concatenate([ends, inner])
    order = jax.random.permutation(jax.random.fold_in(key, 7), SOURCES)
    return joined[order].astype(jnp.int32)


def segment_records(seg_key):
    cable_locations = jnp.arange(WINDOW_TICKS, dtype=jnp.int32)
    noise_key = jax.random.fold_in(seg_key, 1)
    coarse_key = jax.random.fold_in(seg_key, 2)
    phase_key = jax.random.fold_in(seg_key, 3)
    sensor_interval = 8 + 3 * BAND // 4
    sinusoid_tones = []
    for partition_quotient in (2, 4, 8):
        sinusoid_tones.append(WINDOW_TICKS // partition_quotient - sensor_interval)
        sinusoid_tones.append(WINDOW_TICKS // partition_quotient + sensor_interval)
    sensor_total = len(sinusoid_tones)
    background = jax.random.normal(noise_key, (CHANNELS, WINDOW_TICKS), jnp.float32) * noise_scale
    coarse = jax.random.normal(coarse_key, (sensor_total, CHANNELS, BAND + 1), jnp.float32) * envelope_scale
    record_gain = jnp.ones((CHANNELS, 1), jnp.float32)
    phases = jax.random.uniform(phase_key, (sensor_total, CHANNELS), jnp.float32, -math.pi, math.pi)
    scaled = cable_locations * BAND
    lower_index = (scaled // WINDOW_TICKS).astype(jnp.int32)
    upper_index = (lower_index + 1).astype(jnp.int32)
    fraction = (scaled % WINDOW_TICKS).astype(jnp.float32) / WINDOW_TICKS
    combined = background
    for element_ordinal in range(sensor_total):
        lower_value = jnp.take(coarse[element_ordinal], lower_index, axis=1)
        upper_value = jnp.take(coarse[element_ordinal], upper_index, axis=1)
        envelope = lower_value + (upper_value - lower_value) * fraction[None, :]
        cycle_revolutions = (cable_locations * sinusoid_tones[element_ordinal] % WINDOW_TICKS).astype(jnp.float32) * (2.0 * math.pi / WINDOW_TICKS)
        combined = combined + envelope * jnp.cos(cycle_revolutions[None, :] + phases[element_ordinal][:, None])
    return combined * record_gain


def draw_records(key, part):
    alive = (jax.random.randint(jax.random.fold_in(key, 11), (SEGS, CHANNELS), 0, 4) != 0).astype(jnp.float32)
    seg_keys = jax.random.split(jax.random.fold_in(key, 13), SEGS)
    whole = lax.map(segment_records, seg_keys)
    clipped = jnp.clip(whole, -6.0, 6.0) * alive[:, :, None]
    return clipped.astype(jnp.bfloat16)


def set_ends(drawn, rng, smallest, top_value):
    longest = drawn.shape.index(max(drawn.shape))
    spots = []
    for shift in (0, 1):
        where = [jax.random.randint(jax.random.fold_in(rng, axis), (), 0, length) for axis, length in enumerate(drawn.shape)]
        where[longest] = (where[longest] + shift) % drawn.shape[longest]
        spots.append(tuple(where))
    return drawn.at[spots[0]].set(smallest).at[spots[1]].set(top_value)


def setup_inputs(seed: int = 0, part: int = 0) -> dict:
    keys = jax.random.split(jax.random.key(seed), 4)
    part_splits = jax.random.split(jax.random.fold_in(keys[3], part), 4)
    records = draw_records(jax.random.fold_in(jax.random.fold_in(keys[3], part), 71), part)
    valid_flags = set_ends((jax.random.randint(part_splits[1], (SEGS, CHANNELS), 0, 4) < 3).astype(jnp.int32), jax.random.fold_in(part_splits[1], 1), 0, 1)
    source_ids = draw_source_ids(jax.random.fold_in(jax.random.fold_in(keys[3], part), 71), part)
    return dict(records=records, valid_flags=valid_flags, source_ids=source_ids)


lowest_bin = 8
floor_share = 0.05
epsilon = 1e-06

def forward_table(offset, length, samples):
    position = offset + jnp.arange(length, dtype=jnp.int32)
    bins = lowest_bin + jnp.arange(BAND, dtype=jnp.int32)
    phase = position[:, None] * bins[None, :] % samples
    angle = phase.astype(jnp.float32) * (2.0 * math.pi / samples)
    return jnp.concatenate([jnp.cos(angle), -jnp.sin(angle)], axis=1).astype(jnp.bfloat16)

def inverse_table(samples):
    shifts = jnp.arange(2 * HALF_LAG + 1, dtype=jnp.int32) - HALF_LAG
    bins = lowest_bin + jnp.arange(BAND, dtype=jnp.int32)
    phase = bins[:, None] * shifts[None, :] % samples
    angle = phase.astype(jnp.float32) * (2.0 * math.pi / samples)
    factor = 1.0 / math.sqrt(BAND)
    return (jnp.concatenate([jnp.cos(angle), -jnp.sin(angle)], axis=0) * factor).astype(jnp.bfloat16)

def whiten(spectra):
    real_part = spectra[..., :BAND]
    imag_part = spectra[..., BAND:]
    power = real_part * real_part + imag_part * imag_part
    level = lax.optimization_barrier(jnp.mean(power, axis=-1, keepdims=True))
    factor = lax.rsqrt(power + floor_share * level + epsilon)
    return jnp.concatenate([real_part * factor, imag_part * factor], axis=-1).astype(jnp.bfloat16)

def cross_stack(panel, source_weights, receivers, weights):
    highest = lax.Precision.HIGHEST
    src_real = panel[..., :BAND]
    src_imag = panel[..., BAND:]
    rec_real = receivers[..., :BAND]
    rec_imag = receivers[..., BAND:]
    cross_real = jnp.einsum('gsf,gcf->scf', src_real, rec_real, precision=highest) + jnp.einsum('gsf,gcf->scf', src_imag, rec_imag, precision=highest)
    cross_imag = jnp.einsum('gsf,gcf->scf', src_imag, rec_real, precision=highest) - jnp.einsum('gsf,gcf->scf', src_real, rec_imag, precision=highest)
    counts = jnp.einsum('gs,gc->sc', source_weights, weights, precision=highest)
    divisor = jnp.maximum(counts, 1.0)[:, :, None]
    return (jnp.concatenate([cross_real, cross_imag], axis=-1) / divisor).astype(jnp.bfloat16)

def reference(records, valid_flags, source_ids):
    samples = records.shape[2]
    table = forward_table(0, samples, samples)
    spectra = lax.map(lambda segment: jnp.dot(segment, table, preferred_element_type=jnp.float32), records)
    white = whiten(spectra)
    weights = valid_flags.astype(jnp.float32)
    receivers = white.astype(jnp.float32) * weights[:, :, None]
    panel = receivers[:, source_ids, :]
    source_weights = weights[:, source_ids]
    stacked = cross_stack(panel, source_weights, receivers, weights)
    result = jnp.dot(stacked.reshape(-1, 2 * BAND), inverse_table(samples), preferred_element_type=jnp.float32)
    return result.reshape(SOURCES, -1, 2 * HALF_LAG + 1)
```

```python
import math

import jax
import jax.numpy as jnp
import numpy as np
from jax import lax
from jax.experimental import pallas as pl
from jax.experimental.pallas import tpu as pltpu
from jax.sharding import PartitionSpec as P

BAND = 600
HALF_LAG = 500
LAGS = 2 * HALF_LAG + 1
WIDE = 640
LAGS_WIDE = 1024
SPANS = 16
SLOTS = 128
COARSE = 16
STEP = 64
LAG_TILE = 256
LANES = 128

lowest_bin = 8
floor_share = 0.05
epsilon = 1e-06
MESH = pl.DeviceIdType.MESH


def unit(phase, samples, scale=1.0):
    angle = 2.0 * np.pi * (phase % samples) / samples
    return (
        (np.cos(angle) * scale).astype(np.float32),
        (-np.sin(angle) * scale).astype(np.float32),
    )


def forward_parts(samples):
    bins = lowest_bin + np.arange(WIDE, dtype=np.int64)
    keep = (np.arange(WIDE) < BAND).astype(np.float64)
    coarse = np.arange(samples // 4 // STEP, dtype=np.int64) * STEP
    fine = np.arange(STEP, dtype=np.int64)
    sample, column, change = near_ties(samples)
    by_slot = np.zeros((SLOTS, WIDE), np.float32)
    by_slot[:, :SPANS] = column.T
    by_slot[:, SLOTS : SLOTS + SPANS] = change.T
    by_span = np.zeros((SPANS, WIDE), np.float32)
    by_span[:, :SLOTS] = sample
    return np.concatenate(
        (
            *unit(coarse[:, None] * bins[None, :], samples, keep),
            *unit(fine[:, None] * bins[None, :], samples),
            by_slot,
            by_span,
        )
    )


def inverse_parts(samples):
    lags = np.arange(LAGS_WIDE, dtype=np.int64) - HALF_LAG
    coarse = lowest_bin + np.arange(COARSE, dtype=np.int64) * STEP
    fine = np.arange(STEP, dtype=np.int64)
    return np.concatenate(
        (
            *unit(coarse[:, None] * lags[None, :], samples, 1.0 / math.sqrt(BAND)),
            *unit(fine[:, None] * lags[None, :], samples),
        )
    )


def rounded(values):
    return values.astype(np.float32).astype(jnp.bfloat16).astype(np.float32)


def near_ties(samples):
    steps = np.arange(samples)
    single = (steps.astype(np.float32) * np.float32(2.0 * math.pi / samples)).astype(np.float64)
    exact = 2.0 * np.pi * steps / samples
    span = samples // SPANS
    sample = np.full((SPANS, SLOTS), -1, np.int32)
    column = np.full((SPANS, SLOTS), -1, np.int32)
    change = np.zeros((SPANS, SLOTS), np.float32)
    used = np.zeros(SPANS, np.int64)
    phase = np.arange(samples)[:, None] * (lowest_bin + np.arange(BAND))[None, :] % samples
    for wide, (held, folded) in enumerate(
        ((np.cos(single), np.cos(exact)), (-np.sin(single), -np.sin(exact)))
    ):
        difference = rounded(held) - rounded(folded)
        for step in np.nonzero(np.abs(difference) > 1e-6)[0]:
            for n, f in np.argwhere(phase == step):
                g = n // span
                sample[g, used[g]] = n % span
                column[g, used[g]] = wide * WIDE + f
                change[g, used[g]] = difference[step]
                used[g] += 1
    return sample, column, change


def angle_sum(ac, an, bc, bn):
    return ac * bc - an * bn, ac * bn + an * bc


def turned(acc, rows, half):
    def part(j, wide):
        return acc[pl.ds(j * rows, rows), pl.ds(wide * WIDE, WIDE)]

    (low_r, low_i), (high_r, high_i) = ((part(j, 0), part(j, 1)) for j in (0, 1))
    turn = (lowest_bin + lax.broadcasted_iota(jnp.int32, (rows, WIDE), 1)) % 4
    swap_r = jnp.where(turn % 2 == 0, high_r, high_i)
    swap_i = jnp.where(turn % 2 == 0, high_i, -high_r)
    real = low_r + jnp.where(turn < 2, swap_r, -swap_r)
    imag = low_i + jnp.where(turn < 2, swap_i, -swap_i)
    flip = (half == 1) & (turn % 2 == 1)
    return jnp.where(flip, -real, real), jnp.where(flip, -imag, imag)


def whiten_rows(real, imag, flags):
    lane = lax.broadcasted_iota(jnp.int32, real.shape, 1)
    power = real * real + imag * imag
    level = jnp.sum(power, axis=1, keepdims=True) * (1.0 / BAND)
    factor = lax.rsqrt(power + floor_share * level + epsilon)
    weight = flags
    real = jnp.where(lane == BAND, weight, real * factor * weight)
    return real.astype(jnp.bfloat16), (imag * factor * weight).astype(jnp.bfloat16)


def kernel(
    devices, ids_ref, flags_ref, x_hbm, forward_hbm, inverse_hbm, out_ref,
    forward, inverse, recv, table, back, acc, pick, put, whole, share, halves,
    everyone, held, stacked,
    send_sem, recv_sem, own_sem, part_sem, share_sem, half_sem, relay_sem, block_sem,
):
    me = lax.axis_index("chan")
    half, segments, tile, length = recv.shape
    sources, ch_local, _ = out_ref.shape
    rows = segments * tile
    quarter = devices // 4
    chips = half // 2
    coarse = devices * length // 4 // STEP
    side, seat = me // half, me % half
    chip, core = seat // 2, me % 2
    received = recv.reshape(half, rows, length)

    def channels_of(target):
        start = ch_local * (target % 2 * half + target // 2 * 2)
        return x_hbm.at[:, pl.ds(pl.multiple_of(start, tile), tile), :]

    def sending(target, source):
        return pltpu.make_async_remote_copy(
            src_ref=channels_of(target),
            dst_ref=recv.at[source],
            send_sem=send_sem,
            recv_sem=recv_sem.at[source],
            device_id={"chan": side * half + target},
            device_id_type=MESH,
        )

    parts = (
        pltpu.make_async_copy(forward_hbm, forward, part_sem.at[0]),
        pltpu.make_async_copy(inverse_hbm, inverse, part_sem.at[1]),
        pltpu.make_async_copy(channels_of(seat), recv.at[seat], own_sem),
    )
    for part in parts:
        part.start()
    barrier = pltpu.get_barrier_semaphore()
    depth = devices // 8
    z = me // 8
    across = (1 - side) * half + 2 * chip

    def greet(device):
        pl.semaphore_signal(barrier, inc=1, device_id={"chan": device}, device_id_type=MESH)

    greet(across)
    greet(across + 1)

    @pl.when(z == depth // 2 - 1)
    def _():
        greet(me + 8)

    @pl.when(z == depth // 2)
    def _():
        greet(me - 8)

    @pl.loop(1, half)
    def _(r):
        greet(side * half + (seat + r) % half)

    middle = (z == depth // 2 - 1) | (z == depth // 2)

    @pl.when(middle)
    def _():
        pl.semaphore_wait(barrier, half + 2)

    @pl.when(jnp.logical_not(middle))
    def _():
        pl.semaphore_wait(barrier, half + 1)

    for role in (1 - side, side):

        @pl.loop(0, chips)
        def _(k):
            target = 2 * ((chip + chips // 2 + k) % chips) + role

            @pl.when(target != seat)
            def _():
                sending(target, seat).start()

    for part in parts:
        part.wait()

    fine = pl.ds(2 * coarse, STEP), pl.ds(2 * coarse + STEP, STEP)

    @pl.loop(0, coarse)
    def _(a):
        cos, sin = angle_sum(
            forward[pl.ds(a, 1), :],
            forward[pl.ds(coarse + a, 1), :],
            forward[fine[0], :],
            forward[fine[1], :],
        )
        at = pl.ds(pl.multiple_of(a * STEP, STEP), STEP)
        table[at, pl.ds(0, WIDE)] = cos.astype(jnp.bfloat16)
        table[at, pl.ds(WIDE, WIDE)] = sin.astype(jnp.bfloat16)

    span = devices * length // SPANS
    spans = SPANS // 2
    by_slot = 2 * coarse + 2 * STEP
    for g in range(spans):
        by_side = [
            forward[pl.ds(by_slot + SLOTS + first + g, 1), pl.ds(0, SLOTS)]
            for first in (0, spans)
        ]
        sample = jnp.where(side == 0, by_side[0], by_side[1]).astype(jnp.int32)
        here = lax.broadcasted_iota(jnp.int32, (span, SLOTS), 0) == sample
        pick[g] = jnp.where(here, 1.0, 0.0).astype(jnp.bfloat16)
        by_side = [
            forward[pl.ds(by_slot, SLOTS), pl.ds(first + g, 1)]
            for first in (0, spans, SLOTS, SLOTS + spans)
        ]
        column = jnp.where(side == 0, by_side[0], by_side[1]).astype(jnp.int32)
        change = jnp.where(side == 0, by_side[2], by_side[3])
        there = lax.broadcasted_iota(jnp.int32, (SLOTS, 2 * WIDE), 1) == column
        put[pl.ds(g * SLOTS, SLOTS), :] = jnp.where(there, change, 0.0).astype(jnp.bfloat16)

    for a in range(WIDE // STEP):
        cos, sin = angle_sum(
            inverse[pl.ds(a, 1), :],
            inverse[pl.ds(COARSE + a, 1), :],
            inverse[pl.ds(2 * COARSE, STEP), :],
            inverse[pl.ds(2 * COARSE + STEP, STEP), :],
        )
        back[pl.ds(a * STEP, STEP), :] = cos.astype(jnp.bfloat16)
        back[pl.ds(WIDE + a * STEP, STEP), :] = sin.astype(jnp.bfloat16)

    acc[...] = jnp.zeros_like(acc)

    @pl.loop(0, quarter)
    def _(i):
        for j in range(2):
            source = i + j * quarter

            @pl.when(source != seat)
            def _():
                sending(source, source).wait_recv()

        piece = jnp.concatenate([received[i], received[i + quarter]], axis=0)
        acc[...] += jnp.dot(
            piece,
            table[pl.ds(pl.multiple_of(i * length, length), length), :],
            preferred_element_type=jnp.float32,
        )

    per = devices // SPANS
    picked = []
    for g in range(spans):
        piece = jnp.concatenate([received[g * per + t] for t in range(per)], axis=1)
        picked.append(
            jnp.dot(piece, pick[g], preferred_element_type=jnp.float32).astype(jnp.bfloat16)
        )
    ties = jnp.dot(
        jnp.concatenate(picked, axis=1), put[...], preferred_element_type=jnp.float32
    )
    real, imag = turned(acc, rows, side)
    for k in range(2 * WIDE // LANES):
        at = k * LANES
        source = real[:, at : at + LANES] if at < WIDE else imag[:, at - WIDE : at - WIDE + LANES]
        whole[k] = source + ties[:, at : at + LANES]
    for c in range(tile):
        for k in range(2 * WIDE // LANES):
            share[c, :, pl.ds(k * LANES, LANES)] = whole[k, pl.ds(c, segments, stride=tile), :]

    def sharing(target, k):
        return pltpu.make_async_remote_copy(
            src_ref=share.at[pl.ds(k * ch_local, ch_local)],
            dst_ref=halves.at[side],
            send_sem=share_sem,
            recv_sem=half_sem.at[side],
            device_id={"chan": target},
            device_id_type=MESH,
        )

    def arriving(from_side):
        return pltpu.make_async_remote_copy(
            src_ref=share.at[pl.ds(0, ch_local)],
            dst_ref=halves.at[from_side],
            send_sem=share_sem,
            recv_sem=half_sem.at[from_side],
            device_id={"chan": across},
            device_id_type=MESH,
        )

    @pl.when(core == side)
    def _():
        sharing(me + 1 - 2 * core, 1 - core).start()
        for c in range(ch_local):
            halves[side, c] = share[core * ch_local + c]

    @pl.when(core != side)
    def _():
        sharing(across, 0).start()
        sharing(across + 1, 1).start()
        arriving(side).wait_recv()

    arriving(1 - side).wait_recv()

    square = (segments, segments)
    diagonal = lax.broadcasted_iota(jnp.int32, square, 0) == lax.broadcasted_iota(
        jnp.int32, square, 1
    )
    flags = flags_ref[...].astype(jnp.float32)
    flags = jnp.concatenate(
        [
            jnp.sum(jnp.where(diagonal, flags[c : c + 1, :], 0.0), axis=1, keepdims=True)
            for c in range(ch_local)
        ],
        axis=0,
    )
    total = (halves[0] + halves[1]).reshape(ch_local * segments, 2 * WIDE)
    real, imag = whiten_rows(total[:, :WIDE], total[:, WIDE:], flags)
    own_rows = pl.ds(me * ch_local, ch_local)
    everyone[own_rows, :, pl.ds(0, WIDE)] = real.reshape(ch_local, segments, WIDE)
    everyone[own_rows, :, pl.ds(WIDE, WIDE)] = imag.reshape(ch_local, segments, WIDE)

    flip = {bit: me + bit - 2 * bit * (me // bit % 2) for bit in (1, 2, 4)}

    def relay(source, h, target):
        block = everyone.at[source * ch_local + h]
        return pltpu.make_async_remote_copy(
            src_ref=block,
            dst_ref=block,
            send_sem=relay_sem,
            recv_sem=block_sem.at[source, h],
            device_id={"chan": target},
            device_id_type=MESH,
        )

    def each_relay(zs, far, h, act):
        first, second = ((4, 2), (2, 4))[h % 2]
        base = (me, flip[first], flip[second], flip[first] + flip[second] - me)[far]
        source = base + (zs - z) * 8
        if far == 0:

            @pl.when((zs <= z) & (z + 1 < depth))
            def _():
                act(relay(source, h, me + 8))

            @pl.when((zs >= z) & (z > 0))
            def _():
                act(relay(source, h, me - 8))

            act(relay(source, h, flip[first]))
        if far <= 1:
            act(relay(source, h, flip[second]))
        act(relay(source, h, flip[1]))

    def each_block(act):
        @pl.loop(0, depth + 2)
        def _(wave):
            for far, hops in enumerate((0, 1, 1, 2)):
                k = wave - hops
                for side in (-1, 1):
                    zs = z + side * k
                    real_block = (k >= 0) & (k < depth) & (zs >= 0) & (zs < depth)
                    if side == 1:
                        real_block = real_block & (k > 0)

                    @pl.when(real_block)
                    def _():
                        for h in range(ch_local):
                            act(zs, far, h)

    def forward_block(zs, far, h):
        first, second = ((4, 2), (2, 4))[h % 2]
        base = (me, flip[first], flip[second], flip[first] + flip[second] - me)[far]
        source = base + (zs - z) * 8

        @pl.when(source != me)
        def _():
            relay(source, h, me).wait_recv()

        each_relay(zs, far, h, lambda copy: copy.start())

    each_block(forward_block)

    @pl.loop(0, devices // 2)
    def _(r):
        source = 2 * r + flip[1] % 2
        for h in range(ch_local):
            relay(source, h, me).wait_recv()

    group = 8

    @pl.loop(0, sources // group)
    def _(block):
        for s in range(group):
            held[s] = everyone[ids_ref[block * group + s]].astype(jnp.float32)
        lane = lax.broadcasted_iota(jnp.int32, (group, WIDE), 1)
        src_r, src_i = held[:, :, pl.ds(0, WIDE)], held[:, :, pl.ds(WIDE, WIDE)]
        for c in range(ch_local):
            mine = everyone[me * ch_local + c].astype(jnp.float32)
            rec_r, rec_i = mine[None, :, :WIDE], mine[None, :, WIDE:]
            real = jnp.sum(src_r * rec_r + src_i * rec_i, axis=1)
            imag = jnp.sum(src_i * rec_r - src_r * rec_i, axis=1)
            counts = jnp.sum(jnp.where(lane == BAND, real, 0.0), axis=1, keepdims=True)
            divisor = jnp.maximum(counts, 1.0)
            at = pl.ds(block * (group * ch_local) + c, group, stride=ch_local)
            real = jnp.where(lane < BAND, real / divisor, 0.0)
            imag = imag / divisor
            for k in range(WIDE // LANES):
                stacked[k, at, :] = real[:, k * LANES : (k + 1) * LANES]
                stacked[WIDE // LANES + k, at, :] = imag[:, k * LANES : (k + 1) * LANES]

    left = jnp.concatenate(
        [stacked[k].astype(jnp.bfloat16) for k in range(2 * WIDE // LANES)], axis=1
    )
    for first in range(0, LAGS, LAG_TILE):
        lags = jnp.dot(
            left, back[:, pl.ds(first, LAG_TILE)], preferred_element_type=jnp.float32
        )
        lags = lags.reshape(sources, ch_local, LAG_TILE)
        width = min(LAG_TILE, LAGS - first)
        out_ref[:, :, pl.ds(first, width)] = lags[:, :, :width]

    for role in (1 - side, side):

        @pl.loop(0, chips)
        def _(k):
            target = 2 * ((chip + k) % chips) + role

            @pl.when(target != seat)
            def _():
                sending(target, seat).wait_send()

    sharing(me + 1 - 2 * core, 1 - core).wait_send()

    @pl.when(core != side)
    def _():
        sharing(across, 0).wait_send()

    each_block(lambda zs, far, h: each_relay(zs, far, h, lambda copy: copy.wait_send()))


def per_device(records, valid_flags, source_ids):
    devices = lax.axis_size("chan")
    segments, channels, length = records.shape
    ch_local = channels // devices
    rows = ch_local * segments
    samples = length * devices
    sources = source_ids.shape[0]
    forward, inverse = forward_parts(samples), inverse_parts(samples)
    vmem = pl.BlockSpec(memory_space=pltpu.VMEM)
    anywhere = pl.BlockSpec(memory_space=pl.ANY)
    return pl.pallas_call(
        lambda *refs: kernel(devices, *refs),
        out_shape=jax.ShapeDtypeStruct((sources, ch_local, LAGS), jnp.float32),
        in_specs=[pl.BlockSpec(memory_space=pltpu.SMEM), vmem, anywhere, anywhere, anywhere],
        out_specs=vmem,
        scratch_shapes=[
            pltpu.VMEM(forward.shape, jnp.float32),
            pltpu.VMEM(inverse.shape, jnp.float32),
            pltpu.VMEM((devices // 2, segments, 2 * ch_local, length), jnp.bfloat16),
            pltpu.VMEM((samples // 4, 2 * WIDE), jnp.bfloat16),
            pltpu.VMEM((2 * WIDE, LAGS_WIDE), jnp.bfloat16),
            pltpu.VMEM((4 * rows, 2 * WIDE), jnp.float32),
            pltpu.VMEM((SPANS // 2, samples // SPANS, SLOTS), jnp.bfloat16),
            pltpu.VMEM((SPANS // 2 * SLOTS, 2 * WIDE), jnp.bfloat16),
            pltpu.VMEM((2 * WIDE // LANES, 2 * rows, LANES), jnp.float32),
            pltpu.VMEM((2 * ch_local, segments, 2 * WIDE), jnp.float32),
            pltpu.VMEM((2, ch_local, segments, 2 * WIDE), jnp.float32),
            pltpu.VMEM((channels, segments, 2 * WIDE), jnp.bfloat16),
            pltpu.VMEM((8, segments, 2 * WIDE), jnp.float32),
            pltpu.VMEM((2 * WIDE // LANES, ch_local * sources, LANES), jnp.float32),
            pltpu.SemaphoreType.DMA,
            pltpu.SemaphoreType.DMA((devices // 2,)),
            pltpu.SemaphoreType.DMA,
            pltpu.SemaphoreType.DMA((2,)),
            pltpu.SemaphoreType.DMA,
            pltpu.SemaphoreType.DMA((2,)),
            pltpu.SemaphoreType.DMA,
            pltpu.SemaphoreType.DMA((devices, ch_local)),
        ],
        compiler_params=pltpu.CompilerParams(
            collective_id=0, has_side_effects=True, vmem_limit_bytes=56 << 20
        ),
        name="correlate",
    )(source_ids, valid_flags.T, records, jnp.asarray(forward), jnp.asarray(inverse))


def solution(mesh):
    return jax.shard_map(
        per_device,
        mesh=mesh,
        in_specs=(P("group", None, "chan"), P("group", "chan"), P("group")),
        out_specs=P("group", "chan", None),
        check_vma=False,
    )
```

```python
import math

import jax
import jax.numpy as jnp
import numpy as np
from jax import lax
from jax.experimental import pallas as pl
from jax.experimental.pallas import tpu as pltpu
from jax.sharding import PartitionSpec as P

BAND = 600
HALF_LAG = 500
LAGS = 2 * HALF_LAG + 1
WIDE = 640
LAGS_WIDE = 1024
SPANS = 16
SLOTS = 128
COARSE = 16
STEP = 64
LAG_TILE = 256
LANES = 128
PARTS = 2
PAIR = 2

lowest_bin = 8
floor_share = 0.05
epsilon = 1e-06
MESH = pl.DeviceIdType.MESH


def unit(phase, samples, scale=1.0):
    angle = 2.0 * np.pi * (phase % samples) / samples
    return (
        (np.cos(angle) * scale).astype(np.float32),
        (-np.sin(angle) * scale).astype(np.float32),
    )


def forward_parts(samples):
    bins = lowest_bin + np.arange(WIDE, dtype=np.int64)
    keep = (np.arange(WIDE) < BAND).astype(np.float64)
    coarse = np.arange(samples // 4 // STEP, dtype=np.int64) * STEP
    fine = np.arange(STEP, dtype=np.int64)
    sample, column, change = near_ties(samples)
    by_slot = np.zeros((SLOTS, WIDE), np.float32)
    by_slot[:, :SPANS] = column.T
    by_slot[:, SLOTS : SLOTS + SPANS] = change.T
    by_span = np.zeros((SPANS, WIDE), np.float32)
    by_span[:, :SLOTS] = sample
    return np.concatenate(
        (
            *unit(coarse[:, None] * bins[None, :], samples, keep),
            *unit(fine[:, None] * bins[None, :], samples),
            by_slot,
            by_span,
        )
    )


def inverse_parts(samples):
    lags = np.arange(LAGS_WIDE, dtype=np.int64) - HALF_LAG
    coarse = lowest_bin + np.arange(COARSE, dtype=np.int64) * STEP
    fine = np.arange(STEP, dtype=np.int64)
    return np.concatenate(
        (
            *unit(coarse[:, None] * lags[None, :], samples, 1.0 / math.sqrt(BAND)),
            *unit(fine[:, None] * lags[None, :], samples),
        )
    )


def rounded(values):
    return values.astype(np.float32).astype(jnp.bfloat16).astype(np.float32)


def near_ties(samples):
    steps = np.arange(samples)
    single = (steps.astype(np.float32) * np.float32(2.0 * math.pi / samples)).astype(np.float64)
    exact = 2.0 * np.pi * steps / samples
    span = samples // SPANS
    sample = np.full((SPANS, SLOTS), -1, np.int32)
    column = np.full((SPANS, SLOTS), -1, np.int32)
    change = np.zeros((SPANS, SLOTS), np.float32)
    used = np.zeros(SPANS, np.int64)
    phase = np.arange(samples)[:, None] * (lowest_bin + np.arange(BAND))[None, :] % samples
    for wide, (held, folded) in enumerate(
        ((np.cos(single), np.cos(exact)), (-np.sin(single), -np.sin(exact)))
    ):
        difference = rounded(held) - rounded(folded)
        for step in np.nonzero(np.abs(difference) > 1e-6)[0]:
            for n, f in np.argwhere(phase == step):
                g = n // span
                sample[g, used[g]] = n % span
                column[g, used[g]] = wide * WIDE + f
                change[g, used[g]] = difference[step]
                used[g] += 1
    return sample, column, change


def angle_sum(ac, an, bc, bn):
    return ac * bc - an * bn, ac * bn + an * bc


def turned(acc, rows, half):
    def part(j, wide):
        return acc[pl.ds(j * rows, rows), pl.ds(wide * WIDE, WIDE)]

    (low_r, low_i), (high_r, high_i) = ((part(j, 0), part(j, 1)) for j in (0, 1))
    turn = (lowest_bin + lax.broadcasted_iota(jnp.int32, (rows, WIDE), 1)) % 4
    swap_r = jnp.where(turn % 2 == 0, high_r, high_i)
    swap_i = jnp.where(turn % 2 == 0, high_i, -high_r)
    real = low_r + jnp.where(turn < 2, swap_r, -swap_r)
    imag = low_i + jnp.where(turn < 2, swap_i, -swap_i)
    flip = (half == 1) & (turn % 2 == 1)
    return jnp.where(flip, -real, real), jnp.where(flip, -imag, imag)


def whiten_rows(real, imag, flags):
    lane = lax.broadcasted_iota(jnp.int32, real.shape, 1)
    power = real * real + imag * imag
    level = jnp.sum(power, axis=1, keepdims=True) * (1.0 / BAND)
    factor = lax.rsqrt(power + floor_share * level + epsilon)
    weight = flags
    real = jnp.where(lane == BAND, weight, real * factor * weight)
    return real.astype(jnp.bfloat16), (imag * factor * weight).astype(jnp.bfloat16)


def kernel(
    devices, ids_ref, flags_ref, x_hbm, forward_hbm, inverse_hbm, out_ref,
    forward, inverse, recv, table, back, acc, pick, put, whole, share, halves,
    everyone, held, mine, stacked,
    send_sem, recv_sem, own_sem, part_sem, share_sem, half_sem, relay_sem, block_sem,
):
    me = lax.axis_index("chan")
    _, half, segments, tile, length = recv.shape
    sources, ch_local, _ = out_ref.shape
    rows = segments * tile
    quarter = devices // 4
    chips = half // 2
    coarse = devices * length // 4 // STEP
    side, seat = me // half, me % half
    chip, core = seat // 2, me % 2
    received = recv.reshape(PARTS, half, rows, length)

    def channels_of(part, target):
        start = pl.multiple_of(ch_local * (target % 2 * half + target // 2 * 2), tile)
        return x_hbm.at[pl.ds(part * segments, segments), pl.ds(start, tile), :]

    def sending(part, target, source):
        return pltpu.make_async_remote_copy(
            src_ref=channels_of(part, target),
            dst_ref=recv.at[part, source],
            send_sem=send_sem,
            recv_sem=recv_sem.at[part, source],
            device_id={"chan": side * half + target},
            device_id_type=MESH,
        )

    parts = (
        pltpu.make_async_copy(forward_hbm, forward, part_sem.at[0]),
        pltpu.make_async_copy(inverse_hbm, inverse, part_sem.at[1]),
        pltpu.make_async_copy(channels_of(0, seat), recv.at[0, seat], own_sem.at[0]),
        pltpu.make_async_copy(channels_of(1, seat), recv.at[1, seat], own_sem.at[1]),
    )
    for copy in parts:
        copy.start()
    barrier = pltpu.get_barrier_semaphore()
    depth = devices // 8
    z = me // 8
    across = (1 - side) * half + 2 * chip

    def greet(device):
        pl.semaphore_signal(barrier, inc=1, device_id={"chan": device}, device_id_type=MESH)

    greet(across)
    greet(across + 1)

    @pl.when(z == depth // 2 - 1)
    def _():
        greet(me + 8)

    @pl.when(z == depth // 2)
    def _():
        greet(me - 8)

    @pl.loop(1, half)
    def _(r):
        greet(side * half + (seat + r) % half)

    middle = (z == depth // 2 - 1) | (z == depth // 2)

    @pl.when(middle)
    def _():
        pl.semaphore_wait(barrier, half + 2)

    @pl.when(jnp.logical_not(middle))
    def _():
        pl.semaphore_wait(barrier, half + 1)

    def each_sending(act):
        for part in range(PARTS):
            for role in (1 - side, side):

                @pl.loop(0, chips)
                def _(k):
                    target = 2 * ((chip + chips // 2 + k) % chips) + role

                    @pl.when(target != seat)
                    def _():
                        act(sending(part, target, seat))

    each_sending(lambda copy: copy.start())

    for copy in parts:
        copy.wait()

    fine = pl.ds(2 * coarse, STEP), pl.ds(2 * coarse + STEP, STEP)

    @pl.loop(0, coarse)
    def _(a):
        cos, sin = angle_sum(
            forward[pl.ds(a, 1), :],
            forward[pl.ds(coarse + a, 1), :],
            forward[fine[0], :],
            forward[fine[1], :],
        )
        at = pl.ds(pl.multiple_of(a * STEP, STEP), STEP)
        table[at, pl.ds(0, WIDE)] = cos.astype(jnp.bfloat16)
        table[at, pl.ds(WIDE, WIDE)] = sin.astype(jnp.bfloat16)

    span = devices * length // SPANS
    spans = SPANS // 2
    by_slot = 2 * coarse + 2 * STEP
    for g in range(spans):
        by_side = [
            forward[pl.ds(by_slot + SLOTS + first + g, 1), pl.ds(0, SLOTS)]
            for first in (0, spans)
        ]
        sample = jnp.where(side == 0, by_side[0], by_side[1]).astype(jnp.int32)
        here = lax.broadcasted_iota(jnp.int32, (span, SLOTS), 0) == sample
        pick[g] = jnp.where(here, 1.0, 0.0).astype(jnp.bfloat16)
        by_side = [
            forward[pl.ds(by_slot, SLOTS), pl.ds(first + g, 1)]
            for first in (0, spans, SLOTS, SLOTS + spans)
        ]
        column = jnp.where(side == 0, by_side[0], by_side[1]).astype(jnp.int32)
        change = jnp.where(side == 0, by_side[2], by_side[3])
        there = lax.broadcasted_iota(jnp.int32, (SLOTS, 2 * WIDE), 1) == column
        put[pl.ds(g * SLOTS, SLOTS), :] = jnp.where(there, change, 0.0).astype(jnp.bfloat16)

    for a in range(WIDE // STEP):
        cos, sin = angle_sum(
            inverse[pl.ds(a, 1), :],
            inverse[pl.ds(COARSE + a, 1), :],
            inverse[pl.ds(2 * COARSE, STEP), :],
            inverse[pl.ds(2 * COARSE + STEP, STEP), :],
        )
        back[pl.ds(a * STEP, STEP), :] = cos.astype(jnp.bfloat16)
        back[pl.ds(WIDE + a * STEP, STEP), :] = sin.astype(jnp.bfloat16)

    per = devices // SPANS

    def sharing(part, target, k):
        return pltpu.make_async_remote_copy(
            src_ref=share.at[part, pl.ds(k * ch_local, ch_local)],
            dst_ref=halves.at[part, side],
            send_sem=share_sem,
            recv_sem=half_sem.at[part, side],
            device_id={"chan": target},
            device_id_type=MESH,
        )

    def arriving(part, from_side):
        return pltpu.make_async_remote_copy(
            src_ref=share.at[part, pl.ds(0, ch_local)],
            dst_ref=halves.at[part, from_side],
            send_sem=share_sem,
            recv_sem=half_sem.at[part, from_side],
            device_id={"chan": across},
            device_id_type=MESH,
        )

    def transform(part):
        acc[...] = jnp.zeros_like(acc)

        @pl.loop(0, quarter)
        def _(i):
            for j in range(2):
                source = i + j * quarter

                @pl.when(source != seat)
                def _():
                    sending(part, source, source).wait_recv()

            piece = jnp.concatenate([received[part, i], received[part, i + quarter]], axis=0)
            acc[...] += jnp.dot(
                piece,
                table[pl.ds(pl.multiple_of(i * length, length), length), :],
                preferred_element_type=jnp.float32,
            )

        picked = []
        for g in range(spans):
            piece = jnp.concatenate([received[part, g * per + t] for t in range(per)], axis=1)
            picked.append(
                jnp.dot(piece, pick[g], preferred_element_type=jnp.float32).astype(jnp.bfloat16)
            )
        ties = jnp.dot(
            jnp.concatenate(picked, axis=1), put[...], preferred_element_type=jnp.float32
        )
        real, imag = turned(acc, rows, side)
        for k in range(2 * WIDE // LANES):
            at = k * LANES
            source = real[:, at : at + LANES] if at < WIDE else imag[:, at - WIDE : at - WIDE + LANES]
            whole[k] = source + ties[:, at : at + LANES]
        for c in range(tile):
            for k in range(2 * WIDE // LANES):
                share[part, c, :, pl.ds(k * LANES, LANES)] = whole[
                    k, pl.ds(c, segments, stride=tile), :
                ]

        @pl.when(core == side)
        def _():
            sharing(part, me + 1 - 2 * core, 1 - core).start()
            for c in range(ch_local):
                halves[part, side, c] = share[part, core * ch_local + c]

        @pl.when(core != side)
        def _():
            sharing(part, across, 0).start()
            sharing(part, across + 1, 1).start()

    flags = flags_ref[...].astype(jnp.float32)
    square = (segments, PARTS * segments)
    diagonal = lax.broadcasted_iota(jnp.int32, square, 1) - lax.broadcasted_iota(
        jnp.int32, square, 0
    )

    def whiten(part):
        @pl.when(core != side)
        def _():
            arriving(part, side).wait_recv()

        arriving(part, 1 - side).wait_recv()
        for c in range(ch_local):
            total = halves[part, 0, c] + halves[part, 1, c]
            picks = diagonal == part * segments
            weight = jnp.sum(jnp.where(picks, flags[c : c + 1, :], 0.0), axis=1, keepdims=True)
            real, imag = whiten_rows(total[:, :WIDE], total[:, WIDE:], weight)
            everyone[part, me * ch_local + c, :, pl.ds(0, WIDE)] = real
            everyone[part, me * ch_local + c, :, pl.ds(WIDE, WIDE)] = imag

    flip = {bit: me + bit - 2 * bit * (me // bit % 2) for bit in (1, 2, 4)}

    pairs = ch_local // PAIR

    def relay(part, source, h, target):
        block = everyone.at[part, pl.ds(source * ch_local + h * PAIR, PAIR)]
        return pltpu.make_async_remote_copy(
            src_ref=block,
            dst_ref=block,
            send_sem=relay_sem,
            recv_sem=block_sem.at[part, source, h],
            device_id={"chan": target},
            device_id_type=MESH,
        )

    def source_of(zs, far, h):
        first, second = ((4, 2), (2, 4))[h % 2]
        base = (me, flip[first], flip[second], flip[first] + flip[second] - me)[far]
        return base + (zs - z) * 8

    def each_relay(part, zs, far, h, act):
        first, second = ((4, 2), (2, 4))[h % 2]
        source = source_of(zs, far, h)
        if far == 0:

            @pl.when((zs <= z) & (z + 1 < depth))
            def _():
                act(relay(part, source, h, me + 8))

            @pl.when((zs >= z) & (z > 0))
            def _():
                act(relay(part, source, h, me - 8))

            act(relay(part, source, h, flip[first]))
        if far <= 1:
            act(relay(part, source, h, flip[second]))
        act(relay(part, source, h, flip[1]))

    def each_block(lowest, highest, act):
        @pl.loop(lowest, highest)
        def _(wave):
            for far, hops in enumerate((0, 1, 1, 2)):
                k = wave - hops
                for way in (-1, 1):
                    zs = z + way * k
                    real_block = (k >= 0) & (k < depth) & (zs >= 0) & (zs < depth)
                    if way == 1:
                        real_block = real_block & (k > 0)

                    @pl.when(real_block)
                    def _():
                        for h in range(pairs):
                            act(zs, far, h)

    def pass_on(part, lowest, highest):
        def step(zs, far, h):
            source = source_of(zs, far, h)

            @pl.when(source != me)
            def _():
                relay(part, source, h, me).wait_recv()

            each_relay(part, zs, far, h, lambda copy: copy.start())

        each_block(lowest, highest, step)

    transform(0)
    whiten(0)
    pass_on(0, 0, 1)
    transform(1)
    pass_on(0, 1, depth + 2)
    whiten(1)
    pass_on(1, 0, depth + 2)

    for part in range(PARTS):

        @pl.loop(0, devices // 2)
        def _(r):
            source = 2 * r + flip[1] % 2
            for h in range(pairs):
                relay(part, source, h, me).wait_recv()

    for part in range(PARTS):
        for c in range(ch_local):
            at = pl.ds(part * segments, segments)
            mine[c, at, :] = everyone[part, me * ch_local + c].astype(jnp.float32)

    group = 8

    @pl.loop(0, sources // group)
    def _(block):
        for s in range(group):
            for part in range(PARTS):
                at = pl.ds(part * segments, segments)
                held[s, at, :] = everyone[part, ids_ref[block * group + s]].astype(jnp.float32)
        lane = lax.broadcasted_iota(jnp.int32, (group, WIDE), 1)
        src_r, src_i = held[:, :, pl.ds(0, WIDE)], held[:, :, pl.ds(WIDE, WIDE)]
        for c in range(ch_local):
            rec_r, rec_i = mine[c, :, pl.ds(0, WIDE)][None], mine[c, :, pl.ds(WIDE, WIDE)][None]
            real = jnp.sum(src_r * rec_r + src_i * rec_i, axis=1)
            imag = jnp.sum(src_i * rec_r - src_r * rec_i, axis=1)
            counts = jnp.sum(jnp.where(lane == BAND, real, 0.0), axis=1, keepdims=True)
            divisor = jnp.maximum(counts, 1.0)
            at = pl.ds(block * (group * ch_local) + c, group, stride=ch_local)
            real = jnp.where(lane < BAND, real / divisor, 0.0)
            imag = imag / divisor
            for k in range(WIDE // LANES):
                stacked[k, at, :] = real[:, k * LANES : (k + 1) * LANES]
                stacked[WIDE // LANES + k, at, :] = imag[:, k * LANES : (k + 1) * LANES]

    left = jnp.concatenate(
        [stacked[k].astype(jnp.bfloat16) for k in range(2 * WIDE // LANES)], axis=1
    )
    for first in range(0, LAGS, LAG_TILE):
        lags = jnp.dot(
            left, back[:, pl.ds(first, LAG_TILE)], preferred_element_type=jnp.float32
        )
        lags = lags.reshape(sources, ch_local, LAG_TILE)
        width = min(LAG_TILE, LAGS - first)
        out_ref[:, :, pl.ds(first, width)] = lags[:, :, :width]

    each_sending(lambda copy: copy.wait_send())
    for part in range(PARTS):
        sharing(part, me + 1 - 2 * core, 1 - core).wait_send()

        @pl.when(core != side)
        def _():
            sharing(part, across, 0).wait_send()

        each_block(
            0,
            depth + 2,
            lambda zs, far, h: each_relay(part, zs, far, h, lambda copy: copy.wait_send()),
        )


def per_device(records, valid_flags, source_ids):
    devices = lax.axis_size("chan")
    segments, channels, length = records.shape
    ch_local = channels // devices
    short = segments // PARTS
    samples = length * devices
    sources = source_ids.shape[0]
    forward, inverse = forward_parts(samples), inverse_parts(samples)
    vmem = pl.BlockSpec(memory_space=pltpu.VMEM)
    anywhere = pl.BlockSpec(memory_space=pl.ANY)
    return pl.pallas_call(
        lambda *refs: kernel(devices, *refs),
        out_shape=jax.ShapeDtypeStruct((sources, ch_local, LAGS), jnp.float32),
        in_specs=[pl.BlockSpec(memory_space=pltpu.SMEM), vmem, anywhere, anywhere, anywhere],
        out_specs=vmem,
        scratch_shapes=[
            pltpu.VMEM(forward.shape, jnp.float32),
            pltpu.VMEM(inverse.shape, jnp.float32),
            pltpu.VMEM((PARTS, devices // 2, short, 2 * ch_local, length), jnp.bfloat16),
            pltpu.VMEM((samples // 4, 2 * WIDE), jnp.bfloat16),
            pltpu.VMEM((2 * WIDE, LAGS_WIDE), jnp.bfloat16),
            pltpu.VMEM((4 * ch_local * short, 2 * WIDE), jnp.float32),
            pltpu.VMEM((SPANS // 2, samples // SPANS, SLOTS), jnp.bfloat16),
            pltpu.VMEM((SPANS // 2 * SLOTS, 2 * WIDE), jnp.bfloat16),
            pltpu.VMEM((2 * WIDE // LANES, 2 * ch_local * short, LANES), jnp.float32),
            pltpu.VMEM((PARTS, 2 * ch_local, short, 2 * WIDE), jnp.float32),
            pltpu.VMEM((PARTS, 2, ch_local, short, 2 * WIDE), jnp.float32),
            pltpu.VMEM((PARTS, channels, short, 2 * WIDE), jnp.bfloat16),
            pltpu.VMEM((8, segments, 2 * WIDE), jnp.float32),
            pltpu.VMEM((ch_local, segments, 2 * WIDE), jnp.float32),
            pltpu.VMEM((2 * WIDE // LANES, ch_local * sources, LANES), jnp.float32),
            pltpu.SemaphoreType.DMA,
            pltpu.SemaphoreType.DMA((PARTS, devices // 2)),
            pltpu.SemaphoreType.DMA((PARTS,)),
            pltpu.SemaphoreType.DMA((2,)),
            pltpu.SemaphoreType.DMA,
            pltpu.SemaphoreType.DMA((PARTS, 2)),
            pltpu.SemaphoreType.DMA,
            pltpu.SemaphoreType.DMA((PARTS, devices, ch_local // PAIR)),
        ],
        compiler_params=pltpu.CompilerParams(
            collective_id=0, has_side_effects=True, vmem_limit_bytes=56 << 20
        ),
        name="correlate",
    )(source_ids, valid_flags.T, records, jnp.asarray(forward), jnp.asarray(inverse))


def solution(mesh):
    return jax.shard_map(
        per_device,
        mesh=mesh,
        in_specs=(P("group", None, "chan"), P("group", "chan"), P("group")),
        out_specs=P("group", "chan", None),
        check_vma=False,
    )
```
